768 devices in a mesh: dp: 16 (over x, z_lo), tensor: 48 (over z_hi, y, core).
Axes of the slice: x: 4, y: 8, z: 12 (z_hi: 3, z_lo: 4; z = z_hi * 4 + z_lo), core: 2. Of those that a mesh axis runs over, the one named last changes fastest.
Arguments:
- activations: bfloat16 [16384, 6144], P('dp', 'tensor')
- sample_rows: int32 [11264], P('dp'), may hold values from 0 to 1023
- old_factor: float32 [6144, 6144], P('tensor', 'dp'), may hold values from -6 to 6
Outputs:
- new_factor: float32 [6144, 6144], P('tensor', 'dp')
The draws below stay inside these ranges and needn't reach their ends.
Inputs may be any that keep to these rules, and one draw needn't show every extreme that they name: `sample_rows`: each entry indexes one of its own replica's 1024 tokens; repeats may occur.
All inputs are finite; a program needn't handle non-finite values.
Results may differ from the reference program's by a relative error of at most 0.0003.
Values may be sent and summed in bfloat16 or wider, within the bound.
No kernel may reach another device: no remote copies, remote signals or barrier semaphores. Data moves between devices by JAX's collectives and lax.ppermute only.
A program may use at most 32 MiB of HBM per device.

```python
import jax
import jax.numpy as jnp
from jax import lax

FEAT = 6144
ROWS_DEV = 1024
SAMP_DEV = 704
SAMPLES = 11264
N_DP = 16


def draw_activations(key, part):
    rows = N_DP * ROWS_DEV
    keys = jax.random.split(key, 6)
    chan = jnp.exp(jax.random.uniform(keys[0], (1, FEAT), jnp.float32, jnp.log(0.5), jnp.log(3.0)))
    tokscale = jnp.exp(jax.random.uniform(keys[1], (rows, 1), jnp.float32, jnp.log(0.7), jnp.log(1.4)))
    common_tok = jax.random.normal(keys[2], (rows, 1), jnp.float32)
    common_chan = jax.random.normal(keys[3], (1, FEAT), jnp.float32)
    replica = (jnp.arange(rows) // ROWS_DEV).astype(jnp.float32)[:, None]
    jitter = jnp.exp(jax.random.uniform(keys[5], (N_DP, 1), jnp.float32, -0.1, 0.1))
    jitter_rows = jnp.repeat(jitter, ROWS_DEV, axis=0)
    position = replica / float(N_DP - 1)
    noise = jax.random.normal(keys[4], (rows, FEAT), jnp.float32)
    strength = 0.5
    rise = jnp.exp(position * jnp.log(2.0))
    values = rise * jitter_rows * tokscale * chan * (noise + strength * common_tok * common_chan)
    values = jnp.clip(values, -40.0, 40.0)
    return values.astype(jnp.bfloat16)


def plant(result, key, smallest, high):
    extent = result.shape
    index_at = [jax.random.randint(jax.random.fold_in(key, axis), (), 0, extent[axis]) for axis in range(len(extent))]
    result = result.at[tuple(index_at)].set(smallest)
    longest = extent.index(max(extent))
    index_at[longest] = (index_at[longest] + 1) % extent[longest]
    return result.at[tuple(index_at)].set(high)


def levels(stream_key, dims, cuts, smallest, top_value):
    def one(dim, shards_of):
        draws = jax.random.uniform(jax.random.fold_in(jax.random.fold_in(stream_key, 6), dim), (shards_of,), jnp.float32, smallest / len(cuts), top_value / len(cuts))
        return jnp.repeat(jnp.exp(draws), dims[dim] // shards_of).reshape((-1,) + (1,) * (len(dims) - dim - 1))

    level = one(*cuts[0])
    for cut in cuts[1:]:
        level = level * one(*cut)
    return level


def centred(own_key, shape, spread, reach, cuts=(), dtype=jnp.bfloat16):
    factor_of = levels(own_key, shape, cuts, -0.22, 0.18) if cuts else 1.0
    drawn = jax.random.normal(own_key, shape, jnp.float32) * spread * factor_of
    return jnp.minimum(jnp.maximum(drawn, -reach), reach).astype(dtype)


def setup_inputs(seed: int = 0) -> dict:
    streams_of = jax.random.split(jax.random.key(seed), 4)
    return {
        "activations": draw_activations(jax.random.fold_in(streams_of[3], 71), 0),
        "sample_rows": plant(jax.random.randint(streams_of[1], (SAMPLES,), 0, ROWS_DEV), jax.random.fold_in(streams_of[1], 1), 0, ROWS_DEV - 1).astype(jnp.int32),
        "old_factor": centred(streams_of[2], (FEAT, FEAT), 1.0, 6.0, ((0, 48), (1, 16)), jnp.float32),
    }


def reference(activations, sample_rows, old_factor):
    grouped = activations.reshape(N_DP, ROWS_DEV, FEAT)
    picks = sample_rows.reshape(N_DP, SAMP_DEV).astype(jnp.int32)
    sampled = jnp.take_along_axis(grouped, picks[:, :, None], axis=1).reshape(N_DP * SAMP_DEV, FEAT)
    wide = sampled.astype(jnp.float32)
    gram = jnp.dot(wide.T, wide, precision=lax.Precision.HIGHEST, preferred_element_type=jnp.float32)
    return 0.9 * old_factor + 0.1 * gram / jnp.float32(N_DP * SAMP_DEV)
```

```python
import jax
import jax.numpy as jnp
from jax import lax
from jax.experimental import pallas as pl
from jax.experimental.pallas import tpu as pltpu
from jax.sharding import Mesh
from jax.sharding import PartitionSpec as P

NX, NZL, NZH, NY, NC = 4, 4, 3, 8, 2
AXES = ("x", "zl", "zh", "y", "core")


def triple_perm(i):
    return [(3 * w + (i + zh) % 3, zh * 16 + w) for zh in range(NZH) for w in range(16)]


def swap_perm():
    return [
        ((x * NZL + zl) * 16 + w, w * 16 + (2 * x + zl % 2) * NC + zl // 2)
        for x in range(NX)
        for zl in range(NZL)
        for w in range(16)
    ]


def product_kernel(at_ref, a_ref, mine_ref, other_ref, out_ref):
    zh, core = at_ref[0], at_ref[1]
    rows = jnp.concatenate([a_ref[0], a_ref[1]], axis=1)
    for b_ref, cw in ((mine_ref, core), (other_ref, 1 - core)):
        cols = jnp.concatenate(
            [b_ref[lax.rem(j + NZH - zh, NZH)] for j in range(NZH)], axis=1
        )
        out_ref[0, cw] = lax.dot_general(
            rows, cols, (((0,), (0,)), ((), ())), preferred_element_type=jnp.float32
        )


def product(at, a, mine, other):
    k = a.shape[1]
    return pl.pallas_call(
        product_kernel,
        grid_spec=pltpu.PrefetchScalarGridSpec(
            num_scalar_prefetch=1,
            grid=(NX,),
            in_specs=[
                pl.BlockSpec((2, k, 128), lambda i, z: (i, 0, 0)),
                pl.BlockSpec((NZH, k, 128), lambda i, z: (0, 0, 0)),
                pl.BlockSpec((NZH, k, 128), lambda i, z: (0, 0, 0)),
            ],
            out_specs=pl.BlockSpec((1, NC, 256, 384), lambda i, z: (i, 0, 0, 0)),
        ),
        out_shape=jax.ShapeDtypeStruct((NX, NC, 256, 384), jnp.float32),
        cost_estimate=pl.CostEstimate(
            flops=2 * k * 1024 * 768, bytes_accessed=6_000_000, transcendentals=0
        ),
    )(at, a, mine, other)


def body(activations, sample_rows, old_factor):
    block = activations.at[sample_rows].get(mode="promise_in_bounds")
    k = block.shape[0]
    scale = 0.1 / float(NX * NZL * k)
    a = lax.all_gather(block, "y", axis=0)
    mine = jnp.stack([lax.ppermute(block, ("zh", "y", "core"), triple_perm(i)) for i in range(NZH)])
    other = lax.ppermute(mine, "core", [(0, 1), (1, 0)])
    at = jnp.stack([lax.axis_index("zh"), lax.axis_index("core")]).astype(jnp.int32)
    part = product(at, a, mine, other)
    part = lax.all_to_all(
        part.reshape(NX * NC, 256, 384), ("x", "core"), split_axis=0, concat_axis=0, tiled=True
    )
    part = jnp.sum(part.reshape(NX, NZL, 128, 384), axis=0)
    part = lax.all_to_all(part, "zl", split_axis=0, concat_axis=0, tiled=True)
    total = jnp.sum(part, axis=0)
    total = lax.ppermute(total, ("x", "zl", "y", "core"), swap_perm())
    return 0.9 * old_factor + scale * total


def solution(mesh):
    fine = Mesh(mesh.devices.reshape(NX, NZL, NZH, NY, NC), AXES)
    dp, tensor = ("x", "zl"), ("zh", "y", "core")
    return jax.shard_map(
        body,
        mesh=fine,
        in_specs=(P(dp, tensor), P(dp), P(tensor, dp)),
        out_specs=P(tensor, dp),
        check_vma=False,
    )
```

```python
import jax
import jax.numpy as jnp
from jax import lax
from jax.experimental import pallas as pl
from jax.experimental.pallas import tpu as pltpu
from jax.sharding import Mesh
from jax.sharding import PartitionSpec as P

NX, NZL, NZH, NY, NC = 4, 4, 3, 8, 2
AXES = ("x", "zl", "zh", "y", "core")
TRIPLE = ((0, 11), (1, 6), (7, 12), (2, 13), (3, 8), (9, 14), (4, 15), (5, 10))
OFFSET = (((-1, -2), (-3, -4)), ((0, 1), (2, 3)))


def triple_perm(i):
    return [
        (3 * TRIPLE[y][c] + (i + zh) % 3, zh * 16 + y * NC + c)
        for zh in range(NZH)
        for y in range(NY)
        for c in range(NC)
    ]


def ring_perm(cores):
    return [
        (y * NC + c, (y + 1 - 2 * c) % NY * NC + c) for y in range(NY) for c in cores
    ]


def place_perm():
    pairs = []
    for x in range(NX):
        for zl in range(NZL):
            for y in range(NY):
                for c in range(NC):
                    to_y = (y + OFFSET[zl % 2][zl // 2][x // 2]) % NY
                    source = ((x * NZL + zl) * NY + y) * NC + c
                    pairs.append((source, (TRIPLE[y][c] * NY + to_y) * NC + x % 2))
    return pairs


def product_kernel(at_ref, a0_ref, a1_ref, a2_ref, mine_ref, other_ref, out_ref):
    zh, core = at_ref[0], at_ref[1]
    columns = []
    for cw in range(NC):
        for j in range(NZH):
            at = lax.rem(j + NZH - zh, NZH)
            columns.append(jnp.where(core == cw, mine_ref[at], other_ref[at]))
    columns = jnp.concatenate(columns, axis=1)
    for i, (up_ref, down_ref) in enumerate(((a1_ref, a0_ref), (a2_ref, a1_ref))):
        rows = [jnp.where(core == 0, up_ref[c], down_ref[c]) for c in range(NC)]
        out = lax.dot_general(
            jnp.concatenate(rows, axis=1),
            columns,
            (((0,), (0,)), ((), ())),
            preferred_element_type=jnp.float32,
        )
        for c in range(NC):
            for cw in range(NC):
                out_ref[i * NC + c, cw] = out[c * 128 : (c + 1) * 128, cw * 384 : (cw + 1) * 384]


def product(at, a0, a1, a2, mine, other):
    k = a0.shape[1]
    vmem = pl.BlockSpec(memory_space=pltpu.VMEM)
    return pl.pallas_call(
        product_kernel,
        in_specs=[pl.BlockSpec(memory_space=pltpu.SMEM)] + [vmem] * 5,
        out_specs=vmem,
        out_shape=jax.ShapeDtypeStruct((NX, NC, 128, 384), jnp.float32),
        compiler_params=pltpu.CompilerParams(vmem_limit_bytes=32 << 20),
        cost_estimate=pl.CostEstimate(
            flops=2 * k * 512 * 768, bytes_accessed=4_000_000, transcendentals=0
        ),
    )(at, a0, a1, a2, mine, other)


def reduce_x(part):
    part = lax.all_to_all(
        part.reshape(NX * NC, 128, 384), ("x", "core"), split_axis=0, concat_axis=0, tiled=True
    )
    return jnp.sum(part.reshape(NX, NC, 128, 384), axis=0)


def body(activations, sample_rows, old_factor):
    block = activations.at[sample_rows].get(mode="promise_in_bounds")
    scale = 0.1 / float(NX * NZL * block.shape[0])
    at = jnp.stack([lax.axis_index("zh"), lax.axis_index("core")]).astype(jnp.int32)
    ring = [lax.all_gather(block, "core", axis=0)]
    for step in range(4):
        ring.append(lax.ppermute(ring[-1], ("y", "core"), ring_perm((0, 1) if step < 3 else (0,))))
    mine = jnp.stack([lax.ppermute(block, ("zh", "y", "core"), triple_perm(i)) for i in range(NZH)])
    other = lax.ppermute(mine, "core", [(0, 1), (1, 0)])
    halves = [reduce_x(product(at, *ring[2 * h : 2 * h + 3], mine, other)) for h in range(2)]
    part = jnp.concatenate(halves, axis=0)
    part = lax.all_to_all(part, "zl", split_axis=0, concat_axis=0, tiled=True)
    total = jnp.sum(part, axis=0)
    total = lax.ppermute(total, ("x", "zl", "y", "core"), place_perm())
    return 0.9 * old_factor + scale * total


def solution(mesh):
    fine = Mesh(mesh.devices.reshape(NX, NZL, NZH, NY, NC), AXES)
    dp, tensor = ("x", "zl"), ("zh", "y", "core")
    return jax.shard_map(
        body,
        mesh=fine,
        in_specs=(P(dp, tensor), P(dp), P(tensor, dp)),
        out_specs=P(tensor, dp),
        check_vma=False,
    )
```

```python
import math

import jax
import jax.numpy as jnp
from jax import lax
from jax.experimental import pallas as pl
from jax.experimental.pallas import tpu as pltpu
from jax.sharding import Mesh
from jax.sharding import PartitionSpec as P

NX, NZL, NZH, NY, NC = 4, 4, 3, 8, 2
AXES = ("x", "zl", "zh", "y", "core")
TRIPLE = ((0, 11), (1, 6), (7, 12), (2, 13), (3, 8), (9, 14), (4, 15), (5, 10))
OFFSET = (((-1, -2), (-3, -4)), ((0, 1), (2, 3)))
LANES = 128
ROWS = 128
CODED = NZH * ROWS + 16
TOP = 32767.0


def triple_perm(i):
    return [
        (3 * TRIPLE[y][c] + (i + zh) % 3, zh * 16 + y * NC + c)
        for zh in range(NZH)
        for y in range(NY)
        for c in range(NC)
    ]


def ring_perm(cores):
    return [
        (y * NC + c, (y + 1 - 2 * c) % NY * NC + c) for y in range(NY) for c in cores
    ]


def place_perm():
    pairs = []
    for x in range(NX):
        for zl in range(NZL):
            for y in range(NY):
                for c in range(NC):
                    to_y = (y + OFFSET[zl % 2][zl // 2][x // 2]) % NY
                    source = ((x * NZL + zl) * NY + y) * NC + c
                    pairs.append((source, (TRIPLE[y][c] * NY + to_y) * NC + x % 2))
    return pairs


def encode(value, put):
    most = jnp.max(jnp.abs(value), axis=(0, 1), keepdims=True)
    e = jnp.ceil(4.0 / math.log(2.0) * jnp.log(jnp.maximum(most, 2.0**-120)))
    root = jnp.sqrt(jnp.abs(value)) * (TOP * jnp.exp(e * (-math.log(2.0) / 8)))
    q = jnp.where(value < 0, -root, root)
    q = jnp.round(q).astype(jnp.int32).astype(jnp.int16)
    for j in range(NZH):
        put(slice(j * ROWS, (j + 1) * ROWS), q[:, j * LANES : (j + 1) * LANES])
    scale = jnp.broadcast_to(e, (16, LANES)).astype(jnp.int32).astype(jnp.int16)
    put(slice(NZH * ROWS, CODED), scale)


def decode(ref, at):
    e = ref[at, NZH * ROWS : CODED].astype(jnp.int32).astype(jnp.float32)[0:1]
    scale = jnp.exp(e * (math.log(2.0) / 8)) * (1.0 / TOP)
    root = ref[at, 0 : NZH * ROWS].astype(jnp.int32).astype(jnp.float32) * scale
    return root * jnp.abs(root)


def store(ref, *at):
    def put(rows, value):
        ref[(*at, rows)] = value

    return put


def triple_kernel(at_ref, *refs):
    out_ref = refs[NZH]
    for i in range(NZH):
        j = lax.rem(i + at_ref[0], NZH)
        out_ref[:, pl.ds(pl.multiple_of(j * LANES, LANES), LANES)] = refs[i][...]


def product_kernel(at_ref, a0_ref, a1_ref, a2_ref, mine_ref, other_ref, out_ref):
    core = at_ref[1]
    for i, (up_ref, down_ref) in enumerate(((a1_ref, a0_ref), (a2_ref, a1_ref))):
        rows = [jnp.where(core == 0, up_ref[c], down_ref[c]) for c in range(NC)]
        rows = jnp.concatenate(rows, axis=1)
        for columns_ref, cw in ((mine_ref, core), (other_ref, 1 - core)):
            out = lax.dot_general(
                rows, columns_ref[...], (((0,), (0,)), ((), ())), preferred_element_type=jnp.float32
            )
            for c in range(NC):
                encode(out[c * ROWS : (c + 1) * ROWS], store(out_ref, i * NC + c, cw))


def sum_x_kernel(part_ref, out_ref):
    for c in range(NC):
        total = decode(part_ref, c)
        for x in range(1, NX):
            total = total + decode(part_ref, x * NC + c)
        blocks = [total[j * ROWS : (j + 1) * ROWS] for j in range(NZH)]
        encode(jnp.concatenate(blocks, axis=1), store(out_ref, c))


def sum_zl_kernel(part_ref, out_ref):
    total = decode(part_ref, 0)
    for zl in range(1, NZL):
        total = total + decode(part_ref, zl)
    for j in range(NZH):
        out_ref[:, j * LANES : (j + 1) * LANES] = total[j * ROWS : (j + 1) * ROWS]


def call(kernel, shape, dtype, flops, *arrays, scalars=False):
    specs = [pl.BlockSpec(memory_space=pltpu.VMEM)] * (len(arrays) - scalars)
    if scalars:
        specs = [pl.BlockSpec(memory_space=pltpu.SMEM)] + specs
    return pl.pallas_call(
        kernel,
        in_specs=specs,
        out_specs=pl.BlockSpec(memory_space=pltpu.VMEM),
        out_shape=jax.ShapeDtypeStruct(shape, dtype),
        compiler_params=pltpu.CompilerParams(vmem_limit_bytes=24 << 20),
        cost_estimate=pl.CostEstimate(flops=flops, bytes_accessed=2_000_000, transcendentals=0),
    )(*arrays)


def exchange(part, axes):
    return lax.all_to_all(part, axes, split_axis=0, concat_axis=0, tiled=True)


def body(activations, sample_rows, old_factor):
    block = activations.at[sample_rows].get(mode="promise_in_bounds")
    k = block.shape[0]
    scale = 0.1 / float(NX * NZL * k)
    at = jnp.stack([lax.axis_index("zh"), lax.axis_index("core")]).astype(jnp.int32)
    ring = [lax.all_gather(block, "core", axis=0)]
    for step in range(4):
        ring.append(lax.ppermute(ring[-1], ("y", "core"), ring_perm((0, 1) if step < 3 else (0,))))
    block, _ = lax.optimization_barrier((block, ring[0]))
    mine = [lax.ppermute(block, ("zh", "y", "core"), triple_perm(i)) for i in range(NZH)]
    *mine, ring[1] = lax.optimization_barrier((*mine, ring[1]))
    mine = call(triple_kernel, (k, 384), jnp.bfloat16, 0, at, *mine, scalars=True)
    other = lax.ppermute(mine, "core", [(0, 1), (1, 0)])
    part = []
    for half in range(2):
        out = call(
            product_kernel, (NX, NC, CODED, LANES), jnp.int16, 2 * k * 512 * 768,
            at, *ring[2 * half : 2 * half + 3], mine, other, scalars=True,
        )
        out = exchange(out.reshape(NX * NC, CODED, LANES), ("x", "core"))
        part.append(call(sum_x_kernel, (NC, CODED, LANES), jnp.int16, 0, out))
    part = exchange(jnp.concatenate(part, axis=0), "zl")
    total = call(sum_zl_kernel, (ROWS, 384), jnp.float32, 0, part)
    total = lax.ppermute(total, ("x", "zl", "y", "core"), place_perm())
    return 0.9 * old_factor + scale * total


def solution(mesh):
    fine = Mesh(mesh.devices.reshape(NX, NZL, NZH, NY, NC), AXES)
    dp, tensor = ("x", "zl"), ("zh", "y", "core")
    return jax.shard_map(
        body,
        mesh=fine,
        in_specs=(P(dp, tensor), P(dp), P(tensor, dp)),
        out_specs=P(tensor, dp),
        check_vma=False,
    )
```

```python
import math

import jax
import jax.numpy as jnp
from jax import lax
from jax.experimental import pallas as pl
from jax.experimental.pallas import tpu as pltpu
from jax.sharding import Mesh
from jax.sharding import PartitionSpec as P

NX, NZL, NZH, NY, NC = 4, 4, 3, 8, 2
AXES = ("x", "zl", "zh", "y", "core")
TRIPLE = ((0, 11), (1, 6), (7, 12), (2, 13), (3, 8), (9, 14), (4, 15), (5, 10))
OFFSET = (((-1, -2), (-3, -4)), ((0, 1), (2, 3)))
LANES = 128
ROWS = 128
CODED = NZH * ROWS + 16
TOP = 32767.0


def triple_perm(i):
    return [
        (3 * TRIPLE[y][c] + (i + zh) % 3, zh * 16 + y * NC + c)
        for zh in range(NZH)
        for y in range(NY)
        for c in range(NC)
    ]


def ring_perm(cores):
    return [
        (y * NC + c, (y + 1 - 2 * c) % NY * NC + c) for y in range(NY) for c in cores
    ]


def place_perm():
    pairs = []
    for x in range(NX):
        for zl in range(NZL):
            for y in range(NY):
                for c in range(NC):
                    to_y = (y + OFFSET[zl % 2][zl // 2][x // 2]) % NY
                    source = ((x * NZL + zl) * NY + y) * NC + c
                    pairs.append((source, (TRIPLE[y][c] * NY + to_y) * NC + x % 2))
    return pairs


def encode(value, put):
    most = jnp.max(jnp.abs(value), axis=(0, 1), keepdims=True)
    e = jnp.ceil(4.0 / math.log(2.0) * jnp.log(jnp.maximum(most, 2.0**-120)))
    root = jnp.sqrt(jnp.abs(value)) * (TOP * jnp.exp(e * (-math.log(2.0) / 8)))
    q = jnp.where(value < 0, -root, root)
    q = jnp.round(q).astype(jnp.int32).astype(jnp.int16)
    for j in range(NZH):
        put(slice(j * ROWS, (j + 1) * ROWS), q[:, j * LANES : (j + 1) * LANES])
    scale = jnp.broadcast_to(e, (16, LANES)).astype(jnp.int32).astype(jnp.int16)
    put(slice(NZH * ROWS, CODED), scale)


def decode(ref, at):
    e = ref[at, NZH * ROWS : CODED].astype(jnp.int32).astype(jnp.float32)[0:1]
    scale = jnp.exp(e * (math.log(2.0) / 8)) * (1.0 / TOP)
    root = ref[at, 0 : NZH * ROWS].astype(jnp.int32).astype(jnp.float32) * scale
    return root * jnp.abs(root)


def store(ref, *at):
    def put(rows, value):
        ref[(*at, rows)] = value

    return put


def triple_kernel(at_ref, *refs):
    out_ref = refs[NZH]
    for i in range(NZH):
        j = lax.rem(i + at_ref[0], NZH)
        out_ref[:, pl.ds(pl.multiple_of(j * LANES, LANES), LANES)] = refs[i][...]


def product_kernel(at_ref, a0_ref, a1_ref, a2_ref, mine_ref, other_ref, out_ref):
    core = at_ref[1]
    for i, (up_ref, down_ref) in enumerate(((a1_ref, a0_ref), (a2_ref, a1_ref))):
        rows = [jnp.where(core == 0, up_ref[c], down_ref[c]) for c in range(NC)]
        rows = jnp.concatenate(rows, axis=1)
        for columns_ref, cw in ((mine_ref, core), (other_ref, 1 - core)):
            out = lax.dot_general(
                rows, columns_ref[...], (((0,), (0,)), ((), ())), preferred_element_type=jnp.float32
            )
            for c in range(NC):
                encode(out[c * ROWS : (c + 1) * ROWS], store(out_ref, i * NC + c, cw))


def sum_x_kernel(part_ref, *refs):
    out_ref = refs[-1]
    done = out_ref.shape[0] - NC
    for c in range(done):
        out_ref[c] = refs[0][c]
    for c in range(NC):
        total = decode(part_ref, c)
        for x in range(1, NX):
            total = total + decode(part_ref, x * NC + c)
        blocks = [total[j * ROWS : (j + 1) * ROWS] for j in range(NZH)]
        encode(jnp.concatenate(blocks, axis=1), store(out_ref, done + c))


def sum_zl_kernel(part_ref, out_ref):
    total = decode(part_ref, 0)
    for zl in range(1, NZL):
        total = total + decode(part_ref, zl)
    for j in range(NZH):
        out_ref[:, j * LANES : (j + 1) * LANES] = total[j * ROWS : (j + 1) * ROWS]


def call(kernel, shape, dtype, flops, *arrays, scalars=False):
    specs = [pl.BlockSpec(memory_space=pltpu.VMEM)] * (len(arrays) - scalars)
    if scalars:
        specs = [pl.BlockSpec(memory_space=pltpu.SMEM)] + specs
    return pl.pallas_call(
        kernel,
        in_specs=specs,
        out_specs=pl.BlockSpec(memory_space=pltpu.VMEM),
        out_shape=jax.ShapeDtypeStruct(shape, dtype),
        compiler_params=pltpu.CompilerParams(vmem_limit_bytes=24 << 20),
        cost_estimate=pl.CostEstimate(flops=flops, bytes_accessed=2_000_000, transcendentals=0),
    )(*arrays)


def exchange(part, axes):
    return lax.all_to_all(part, axes, split_axis=0, concat_axis=0, tiled=True)


def body(activations, sample_rows, old_factor):
    block = activations.at[sample_rows].get(mode="promise_in_bounds")
    k = block.shape[0]
    scale = 0.1 / float(NX * NZL * k)
    at = jnp.stack([lax.axis_index("zh"), lax.axis_index("core")]).astype(jnp.int32)
    ring = [lax.all_gather(block, "core", axis=0)]
    for step in range(4):
        ring.append(lax.ppermute(ring[-1], ("y", "core"), ring_perm((0, 1) if step < 3 else (0,))))
    block, _ = lax.optimization_barrier((block, ring[0]))
    mine = [lax.ppermute(block, ("zh", "y", "core"), triple_perm(i)) for i in range(NZH)]
    mine = call(triple_kernel, (k, 384), jnp.bfloat16, 10**10, at, *mine, scalars=True)
    mine, ring[2] = lax.optimization_barrier((mine, ring[2]))
    other = lax.ppermute(mine, "core", [(0, 1), (1, 0)])
    part = []
    for half in range(2):
        out = call(
            product_kernel, (NX, NC, CODED, LANES), jnp.int16, 2 * k * 512 * 768,
            at, *ring[2 * half : 2 * half + 3], mine, other, scalars=True,
        )
        out = exchange(out.reshape(NX * NC, CODED, LANES), ("x", "core"))
        part = [call(sum_x_kernel, (NC * (half + 1), CODED, LANES), jnp.int16, 0, out, *part)]
    part = exchange(part[0], "zl")
    total = call(sum_zl_kernel, (ROWS, 384), jnp.float32, 0, part)
    total = lax.ppermute(total, ("x", "zl", "y", "core"), place_perm())
    return 0.9 * old_factor + scale * total


def solution(mesh):
    fine = Mesh(mesh.devices.reshape(NX, NZL, NZH, NY, NC), AXES)
    dp, tensor = ("x", "zl"), ("zh", "y", "core")
    return jax.shard_map(
        body,
        mesh=fine,
        in_specs=(P(dp, tensor), P(dp), P(tensor, dp)),
        out_specs=P(tensor, dp),
        check_vma=False,
    )
```

```python
import math

import jax
import jax.numpy as jnp
from jax import lax
from jax.experimental import pallas as pl
from jax.experimental.pallas import tpu as pltpu
from jax.sharding import Mesh
from jax.sharding import PartitionSpec as P

NX, NZL, NZH, NY, NC = 4, 4, 3, 8, 2
AXES = ("x", "zl", "zh", "y", "core")
TRIPLE = ((0, 11), (1, 6), (7, 12), (2, 13), (3, 8), (9, 14), (4, 15), (5, 10))
OFFSET = (((-1, -2), (-3, -4)), ((0, 1), (2, 3)))
LANES = 128
ROWS = 128
CODED = NZH * ROWS + 16
TOP = 32767.0


def triple_perm(i):
    return [
        (3 * TRIPLE[y][c] + (i + zh) % 3, zh * 16 + y * NC + c)
        for zh in range(NZH)
        for y in range(NY)
        for c in range(NC)
    ]


def ring_perm(cores):
    return [
        (y * NC + c, (y + 1 - 2 * c) % NY * NC + c) for y in range(NY) for c in cores
    ]


def place_perm():
    pairs = []
    for x in range(NX):
        for zl in range(NZL):
            for y in range(NY):
                for c in range(NC):
                    to_y = (y + OFFSET[c][zl // 2][x // 2]) % NY
                    source = ((x * NZL + zl) * NY + y) * NC + c
                    pairs.append((source, (TRIPLE[y][zl % 2] * NY + to_y) * NC + x % 2))
    return pairs


def encode(value, put):
    most = jnp.max(jnp.abs(value), axis=(0, 1), keepdims=True)
    e = jnp.ceil(4.0 / math.log(2.0) * jnp.log(jnp.maximum(most, 2.0**-120)))
    root = jnp.sqrt(jnp.abs(value)) * (TOP * jnp.exp(e * (-math.log(2.0) / 8)))
    q = jnp.where(value < 0, -root, root)
    q = jnp.round(q).astype(jnp.int32).astype(jnp.int16)
    for j in range(NZH):
        put(slice(j * ROWS, (j + 1) * ROWS), q[:, j * LANES : (j + 1) * LANES])
    scale = jnp.broadcast_to(e, (16, LANES)).astype(jnp.int32).astype(jnp.int16)
    put(slice(NZH * ROWS, CODED), scale)


def decode(ref, at):
    e = ref[at, NZH * ROWS : CODED].astype(jnp.int32).astype(jnp.float32)[0:1]
    scale = jnp.exp(e * (math.log(2.0) / 8)) * (1.0 / TOP)
    root = ref[at, 0 : NZH * ROWS].astype(jnp.int32).astype(jnp.float32) * scale
    return root * jnp.abs(root)


def store(ref, *at):
    def put(rows, value):
        ref[(*at, rows)] = value

    return put


def triple_kernel(at_ref, *refs):
    out_ref = refs[NZH]
    for i in range(NZH):
        j = lax.rem(i + at_ref[0], NZH)
        out_ref[:, pl.ds(pl.multiple_of(j * LANES, LANES), LANES)] = refs[i][...]


def product_kernel(at_ref, a0_ref, a1_ref, a2_ref, mine_ref, other_ref, out_ref):
    core = at_ref[1]
    for i, (up_ref, down_ref) in enumerate(((a1_ref, a0_ref), (a2_ref, a1_ref))):
        rows = [jnp.where(core == 0, up_ref[c], down_ref[c]) for c in range(NC)]
        rows = jnp.concatenate(rows, axis=1)
        for columns_ref, cw in ((mine_ref, core), (other_ref, 1 - core)):
            out = lax.dot_general(
                rows, columns_ref[...], (((0,), (0,)), ((), ())), preferred_element_type=jnp.float32
            )
            for c in range(NC):
                encode(out[c * ROWS : (c + 1) * ROWS], store(out_ref, i * NC + c, cw))


def sum_x_kernel(part_ref, *refs):
    out_ref = refs[-1]
    done = out_ref.shape[0] - NC
    for c in range(done):
        out_ref[c] = refs[0][c]
    for c in range(NC):
        total = decode(part_ref, c)
        for x in range(1, NX):
            total = total + decode(part_ref, x * NC + c)
        blocks = [total[j * ROWS : (j + 1) * ROWS] for j in range(NZH)]
        encode(jnp.concatenate(blocks, axis=1), store(out_ref, done + c))


def sum_zl_kernel(part_ref, out_ref):
    total = decode(part_ref, 0)
    for zl in range(1, NZL):
        total = total + decode(part_ref, zl)
    for j in range(NZH):
        out_ref[:, j * LANES : (j + 1) * LANES] = total[j * ROWS : (j + 1) * ROWS]


def call(kernel, shape, dtype, flops, *arrays, scalars=False):
    specs = [pl.BlockSpec(memory_space=pltpu.VMEM)] * (len(arrays) - scalars)
    if scalars:
        specs = [pl.BlockSpec(memory_space=pltpu.SMEM)] + specs
    return pl.pallas_call(
        kernel,
        in_specs=specs,
        out_specs=pl.BlockSpec(memory_space=pltpu.VMEM),
        out_shape=jax.ShapeDtypeStruct(shape, dtype),
        compiler_params=pltpu.CompilerParams(vmem_limit_bytes=24 << 20),
        cost_estimate=pl.CostEstimate(flops=flops, bytes_accessed=2_000_000, transcendentals=0),
    )(*arrays)


def exchange(part, axes):
    return lax.all_to_all(part, axes, split_axis=0, concat_axis=0, tiled=True)


def body(activations, sample_rows, old_factor):
    block = activations.at[sample_rows].get(mode="promise_in_bounds")
    k = block.shape[0]
    scale = 0.1 / float(NX * NZL * k)
    at = jnp.stack([lax.axis_index("zh"), lax.axis_index("core")]).astype(jnp.int32)
    ring = [lax.all_gather(block, "core", axis=0)]
    for step in range(4):
        ring.append(lax.ppermute(ring[-1], ("y", "core"), ring_perm((0, 1) if step < 3 else (0,))))
    block, _ = lax.optimization_barrier((block, ring[0]))
    mine = [lax.ppermute(block, ("zh", "y", "core"), triple_perm(i)) for i in range(NZH)]
    mine = call(triple_kernel, (k, 384), jnp.bfloat16, 10**10, at, *mine, scalars=True)
    mine, ring[2] = lax.optimization_barrier((mine, ring[2]))
    other = lax.ppermute(mine, "core", [(0, 1), (1, 0)])
    part = []
    for half in range(2):
        out = call(
            product_kernel, (NX, NC, CODED, LANES), jnp.int16, 2 * k * 512 * 768,
            at, *ring[2 * half : 2 * half + 3], mine, other, scalars=True,
        )
        out = exchange(out.reshape(NX * NC, CODED, LANES), "x")
        part = [call(sum_x_kernel, (NC * (half + 1), CODED, LANES), jnp.int16, 0, out, *part)]
    part = exchange(part[0], "zl")
    total = call(sum_zl_kernel, (ROWS, 384), jnp.float32, 0, part)
    total = lax.ppermute(total, ("x", "zl", "y", "core"), place_perm())
    return 0.9 * old_factor + scale * total


def solution(mesh):
    fine = Mesh(mesh.devices.reshape(NX, NZL, NZH, NY, NC), AXES)
    dp, tensor = ("x", "zl"), ("zh", "y", "core")
    return jax.shard_map(
        body,
        mesh=fine,
        in_specs=(P(dp, tensor), P(dp), P(tensor, dp)),
        out_specs=P(tensor, dp),
        check_vma=False,
    )
```

```python
import functools
import math

import jax
import jax.numpy as jnp
from jax import lax
from jax.experimental import pallas as pl
from jax.experimental.pallas import tpu as pltpu
from jax.sharding import Mesh
from jax.sharding import PartitionSpec as P

NX, NZL, NZH, NY, NC = 4, 4, 3, 8, 2
AXES = ("x", "zl", "zh", "y", "core")
TRIPLE = ((0, 11), (1, 6), (7, 12), (2, 13), (3, 8), (9, 14), (4, 15), (5, 10))
OFFSET = (((-1, -2), (-3, -4)), ((0, 1), (2, 3)))
LANES = 128
ROWS = 128
CODED = NZH * ROWS + 16
TOP = 32767.0


def triple_perm(i):
    return [
        (3 * TRIPLE[y][c] + (i + zh) % 3, zh * 16 + y * NC + c)
        for zh in range(NZH)
        for y in range(NY)
        for c in range(NC)
    ]


def ring_perm(cores):
    return [
        (y * NC + c, (y + 1 - 2 * c) % NY * NC + c) for y in range(NY) for c in cores
    ]


def place_perm(half, turn):
    pairs = []
    for x in range(NX):
        for zl, cw in ((turn, 0), ((turn + 2) % NZL, 1)):
            for y in range(NY):
                for c in range(NC):
                    to_y = (y + OFFSET[c][half][x // 2]) % NY
                    source = ((x * NZL + zl) * NY + y) * NC + c
                    pairs.append((source, (TRIPLE[y][cw] * NY + to_y) * NC + x % 2))
    return pairs


def encode(value, put):
    most = jnp.max(jnp.abs(value), axis=(0, 1), keepdims=True)
    e = jnp.ceil(4.0 / math.log(2.0) * jnp.log(jnp.maximum(most, 2.0**-120)))
    root = jnp.sqrt(jnp.abs(value)) * (TOP * jnp.exp(e * (-math.log(2.0) / 8)))
    q = jnp.where(value < 0, -root, root)
    q = jnp.round(q).astype(jnp.int32).astype(jnp.int16)
    for j in range(NZH):
        put(slice(j * ROWS, (j + 1) * ROWS), q[:, j * LANES : (j + 1) * LANES])
    scale = jnp.broadcast_to(e, (16, LANES)).astype(jnp.int32).astype(jnp.int16)
    put(slice(NZH * ROWS, CODED), scale)


def decode(ref, *at):
    e = ref[(*at, slice(NZH * ROWS, CODED))].astype(jnp.int32).astype(jnp.float32)[0:1]
    scale = jnp.exp(e * (math.log(2.0) / 8)) * (1.0 / TOP)
    root = ref[(*at, slice(0, NZH * ROWS))].astype(jnp.int32).astype(jnp.float32) * scale
    return root * jnp.abs(root)


def store(ref, *at):
    def put(rows, value):
        ref[(*at, rows)] = value

    return put


def triple_kernel(at_ref, *refs):
    out_ref = refs[NZH]
    for i in range(NZH):
        j = lax.rem(i + at_ref[0], NZH)
        out_ref[:, pl.ds(pl.multiple_of(j * LANES, LANES), LANES)] = refs[i][...]


def product_kernel(at_ref, a0_ref, a1_ref, a2_ref, mine_ref, other_ref, out_ref):
    core = at_ref[1]
    for i, (up_ref, down_ref) in enumerate(((a1_ref, a0_ref), (a2_ref, a1_ref))):
        rows = [jnp.where(core == 0, up_ref[c], down_ref[c]) for c in range(NC)]
        rows = jnp.concatenate(rows, axis=1)
        for columns_ref, cw in ((mine_ref, core), (other_ref, 1 - core)):
            out = lax.dot_general(
                rows, columns_ref[...], (((0,), (0,)), ((), ())), preferred_element_type=jnp.float32
            )
            for c in range(NC):
                encode(out[c * ROWS : (c + 1) * ROWS], store(out_ref, i * NC + c, cw))


def sum_x_kernel(at_ref, part_ref, first_ref, second_ref):
    for out_ref, cw in ((first_ref, at_ref[2]), (second_ref, 1 - at_ref[2])):
        total = decode(part_ref, cw)
        for x in range(1, NX):
            total = total + decode(part_ref, x * NC + cw)
        blocks = [total[j * ROWS : (j + 1) * ROWS] for j in range(NZH)]
        encode(jnp.concatenate(blocks, axis=1), store(out_ref))


def sum_zl_kernel(*refs):
    *part, out_ref = refs
    total = decode(part[0])
    for ref in part[1:]:
        total = total + decode(ref)
    out_ref[...] = total


def update_kernel(scale, *refs):
    *part, first_ref, old_ref, out_ref = refs
    total = first_ref[...]
    for ref in part:
        total = total + decode(ref)
    for j in range(NZH):
        at = slice(j * LANES, (j + 1) * LANES)
        out_ref[:, at] = 0.9 * old_ref[:, at] + scale * total[j * ROWS : (j + 1) * ROWS]


def call(kernel, out, flops, *arrays, scalars=False):
    specs = [pl.BlockSpec(memory_space=pltpu.VMEM)] * (len(arrays) - scalars)
    if scalars:
        specs = [pl.BlockSpec(memory_space=pltpu.SMEM)] + specs
    return pl.pallas_call(
        kernel,
        in_specs=specs,
        out_specs=jax.tree.map(lambda _: pl.BlockSpec(memory_space=pltpu.VMEM), out),
        out_shape=out,
        compiler_params=pltpu.CompilerParams(vmem_limit_bytes=24 << 20),
        cost_estimate=pl.CostEstimate(flops=flops, bytes_accessed=2_000_000, transcendentals=0),
    )(*arrays)


def exchange(part, axes):
    return lax.all_to_all(part, axes, split_axis=0, concat_axis=0, tiled=True)


def body(activations, sample_rows, old_factor):
    array = jax.ShapeDtypeStruct
    block = activations.at[sample_rows].get(mode="promise_in_bounds")
    k = block.shape[0]
    scale = 0.1 / float(NX * NZL * k)
    at = [lax.axis_index("zh"), lax.axis_index("core"), lax.axis_index("zl") // 2]
    at = jnp.stack(at).astype(jnp.int32)
    ring = [lax.all_gather(block, "core", axis=0)]
    for step in range(4):
        ring.append(lax.ppermute(ring[-1], ("y", "core"), ring_perm((0, 1) if step < 3 else (0,))))
    block, _ = lax.optimization_barrier((block, ring[0]))
    mine = [lax.ppermute(block, ("zh", "y", "core"), triple_perm(i)) for i in range(NZH)]
    mine = call(triple_kernel, array((k, 384), jnp.bfloat16), 10**10, at, *mine, scalars=True)
    mine, ring[2] = lax.optimization_barrier((mine, ring[2]))
    other = lax.ppermute(mine, "core", [(0, 1), (1, 0)])
    placed = []
    for half in range(2):
        out = call(
            product_kernel, array((NX, NC, CODED, LANES), jnp.int16), 2 * k * 512 * 768,
            at, *ring[2 * half : 2 * half + 3], mine, other, scalars=True,
        )
        out = exchange(out.reshape(NX * NC, CODED, LANES), "x")
        out = call(sum_x_kernel, (array((CODED, LANES), jnp.int16),) * 2, 0, at, out, scalars=True)
        placed.append([
            lax.ppermute(out[turn // 2], ("x", "zl", "y", "core"), place_perm(half, turn))
            for turn in range(NZL)
        ])
    total = call(sum_zl_kernel, array((NZH * ROWS, LANES), jnp.float32), 0, *placed[0])
    return call(
        functools.partial(update_kernel, scale), array((ROWS, 384), jnp.float32), 0,
        *placed[1], total, old_factor,
    )


def solution(mesh):
    fine = Mesh(mesh.devices.reshape(NX, NZL, NZH, NY, NC), AXES)
    dp, tensor = ("x", "zl"), ("zh", "y", "core")
    return jax.shard_map(
        body,
        mesh=fine,
        in_specs=(P(dp, tensor), P(dp), P(tensor, dp)),
        out_specs=P(tensor, dp),
        check_vma=False,
    )
```

```python
import functools
import math

import jax
import jax.numpy as jnp
from jax import lax
from jax.experimental import pallas as pl
from jax.experimental.pallas import tpu as pltpu
from jax.sharding import Mesh
from jax.sharding import PartitionSpec as P

NX, NZL, NZH, NY, NC = 4, 4, 3, 8, 2
AXES = ("x", "zl", "zh", "y", "core")
TRIPLE = ((0, 11), (1, 6), (7, 12), (2, 13), (3, 8), (9, 14), (4, 15), (5, 10))
OFFSET = (((-1, -2), (-3, -4)), ((0, 1), (2, 3)))
LANES = 128
ROWS = 128
TILE = 16
CODED = NZH * ROWS + TILE
TOP = 32767.0


def triple_perm(i):
    return [
        (3 * TRIPLE[y][c] + (i + zh) % 3, zh * 16 + y * NC + c)
        for zh in range(NZH)
        for y in range(NY)
        for c in range(NC)
    ]


def ring_perm(cores):
    return [
        (y * NC + c, (y + 1 - 2 * c) % NY * NC + c) for y in range(NY) for c in cores
    ]


def place_perm():
    pairs = []
    for x in range(NX):
        for zl in range(NZL):
            for y in range(NY):
                for c in range(NC):
                    to_y = (y + OFFSET[c][zl // 2][x // 2]) % NY
                    source = ((x * NZL + zl) * NY + y) * NC + c
                    pairs.append((source, (TRIPLE[y][zl % 2] * NY + to_y) * NC + x % 2))
    return pairs


def encode(blocks, put):
    row = lax.broadcasted_iota(jnp.int32, (TILE, LANES), 0)
    scales = jnp.zeros((TILE, LANES), jnp.float32)
    for j, value in enumerate(blocks):
        size = jnp.abs(value)
        most = jnp.maximum(jnp.max(size, axis=0, keepdims=True), 2.0**-120)
        e = jnp.ceil(4.0 / math.log(2.0) * jnp.log(most))
        root = jnp.sqrt(size) * (TOP * jnp.exp(e * (-math.log(2.0) / 8)))
        q = jnp.round(jnp.where(value < 0, -root, root))
        put(slice(j * ROWS, (j + 1) * ROWS), q.astype(jnp.int32).astype(jnp.int16))
        scales = jnp.where(row == j, e, scales)
    put(slice(NZH * ROWS, CODED), scales.astype(jnp.int32).astype(jnp.int16))


def decode(ref, *at):
    e = ref[(*at, slice(NZH * ROWS, CODED))].astype(jnp.int32).astype(jnp.float32)
    scales = jnp.exp(e * (math.log(2.0) / 8)) * (1.0 / TOP)
    blocks = []
    for j in range(NZH):
        root = ref[(*at, slice(j * ROWS, (j + 1) * ROWS))].astype(jnp.int32).astype(jnp.float32)
        root = root * scales[j : j + 1]
        blocks.append(root * jnp.abs(root))
    return blocks


def decoded_sum(ref, at):
    total = decode(ref, at[0])
    for i in at[1:]:
        total = [a + b for a, b in zip(total, decode(ref, i))]
    return total


def lane_blocks(value):
    return [value[:, j * LANES : (j + 1) * LANES] for j in range(NZH)]


def store(ref, *at):
    def put(rows, value):
        ref[(*at, rows)] = value

    return put


def triple_kernel(at_ref, *refs):
    out_ref = refs[NZH]
    for i in range(NZH):
        j = lax.rem(i + at_ref[0], NZH)
        out_ref[:, pl.ds(pl.multiple_of(j * LANES, LANES), LANES)] = refs[i][...]


def product_kernel(at_ref, a0_ref, a1_ref, a2_ref, mine_ref, other_ref, out_ref):
    core = at_ref[1]
    for i, (up_ref, down_ref) in enumerate(((a1_ref, a0_ref), (a2_ref, a1_ref))):
        rows = [jnp.where(core == 0, up_ref[c], down_ref[c]) for c in range(NC)]
        rows = jnp.concatenate(rows, axis=1)
        for columns_ref, cw in ((mine_ref, core), (other_ref, 1 - core)):
            out = lax.dot_general(
                rows, columns_ref[...], (((0,), (0,)), ((), ())), preferred_element_type=jnp.float32
            )
            for c in range(NC):
                encode(lane_blocks(out[c * ROWS : (c + 1) * ROWS]), store(out_ref, i * NC + c, cw))


def sum_x_kernel(part_ref, *refs):
    out_ref = refs[-1]
    done = out_ref.shape[0] - NC
    for c in range(done):
        out_ref[c] = refs[0][c]
    for c in range(NC):
        total = decoded_sum(part_ref, [x * NC + c for x in range(NX)])
        encode(total, store(out_ref, done + c))


def sum_zl_kernel(part_ref, out_ref):
    encode(decoded_sum(part_ref, range(NZL)), store(out_ref))


def update_kernel(scale, total_ref, old_ref, out_ref):
    for j, total in enumerate(decode(total_ref)):
        at = slice(j * LANES, (j + 1) * LANES)
        out_ref[:, at] = 0.9 * old_ref[:, at] + scale * total


def call(kernel, shape, dtype, flops, *arrays, scalars=False):
    specs = [pl.BlockSpec(memory_space=pltpu.VMEM)] * (len(arrays) - scalars)
    if scalars:
        specs = [pl.BlockSpec(memory_space=pltpu.SMEM)] + specs
    return pl.pallas_call(
        kernel,
        in_specs=specs,
        out_specs=pl.BlockSpec(memory_space=pltpu.VMEM),
        out_shape=jax.ShapeDtypeStruct(shape, dtype),
        compiler_params=pltpu.CompilerParams(vmem_limit_bytes=24 << 20),
        cost_estimate=pl.CostEstimate(flops=flops, bytes_accessed=2_000_000, transcendentals=0),
    )(*arrays)


def exchange(part, axes):
    return lax.all_to_all(part, axes, split_axis=0, concat_axis=0, tiled=True)


def body(activations, sample_rows, old_factor):
    block = activations.at[sample_rows].get(mode="promise_in_bounds")
    k = block.shape[0]
    scale = 0.1 / float(NX * NZL * k)
    at = jnp.stack([lax.axis_index("zh"), lax.axis_index("core")]).astype(jnp.int32)
    ring = [lax.all_gather(block, "core", axis=0)]
    for step in range(4):
        ring.append(lax.ppermute(ring[-1], ("y", "core"), ring_perm((0, 1) if step < 3 else (0,))))
    block, _ = lax.optimization_barrier((block, ring[0]))
    mine = [lax.ppermute(block, ("zh", "y", "core"), triple_perm(i)) for i in range(NZH)]
    mine = call(triple_kernel, (k, 384), jnp.bfloat16, 10**10, at, *mine, scalars=True)
    mine, ring[2] = lax.optimization_barrier((mine, ring[2]))
    other = lax.ppermute(mine, "core", [(0, 1), (1, 0)])
    part = []
    for half in range(2):
        out = call(
            product_kernel, (NX, NC, CODED, LANES), jnp.int16, 2 * k * 512 * 768,
            at, *ring[2 * half : 2 * half + 3], mine, other, scalars=True,
        )
        out = exchange(out.reshape(NX * NC, CODED, LANES), "x")
        part = [call(sum_x_kernel, (NC * (half + 1), CODED, LANES), jnp.int16, 0, out, *part)]
    part = exchange(part[0], "zl")
    total = call(sum_zl_kernel, (CODED, LANES), jnp.int16, 0, part)
    total = lax.ppermute(total, ("x", "zl", "y", "core"), place_perm())
    return call(
        functools.partial(update_kernel, scale), old_factor.shape, jnp.float32, 0, total, old_factor
    )


def solution(mesh):
    fine = Mesh(mesh.devices.reshape(NX, NZL, NZH, NY, NC), AXES)
    dp, tensor = ("x", "zl"), ("zh", "y", "core")
    return jax.shard_map(
        body,
        mesh=fine,
        in_specs=(P(dp, tensor), P(dp), P(tensor, dp)),
        out_specs=P(tensor, dp),
        check_vma=False,
    )
```

```python
import functools
import math

import jax
import jax.numpy as jnp
from jax import lax
from jax.experimental import pallas as pl
from jax.experimental.pallas import tpu as pltpu
from jax.sharding import Mesh
from jax.sharding import PartitionSpec as P

NX, NZL, NZH, NY, NC = 4, 4, 3, 8, 2
AXES = ("x", "zl", "zh", "y", "core")
TRIPLE = ((0, 11), (1, 6), (7, 12), (2, 13), (3, 8), (9, 14), (4, 15), (5, 10))
OFFSET = (
    (((-1, 0), (1, -2)), ((2, -3), (4, 3))),
    (((1, 0), (-1, 2)), ((-2, 3), (4, -3))),
)
LANES = 128
ROWS = 128
TILE = 16
CODED = NZH * ROWS + TILE
TOP = 32767.0
COST = (10**10, 4*10**9, 10**9, 10**10)


def triple_perm(i):
    return [
        (3 * TRIPLE[y][c] + (i + zh) % 3, zh * 16 + y * NC + c)
        for zh in range(NZH)
        for y in range(NY)
        for c in range(NC)
    ]


def ring_perm():
    return [(y * NC + c, (y + 1 - 2 * c) % NY * NC + c) for y in range(NY) for c in range(NC)]


def place_perm():
    pairs = []
    for x in range(NX):
        for zl in range(NZL):
            for y in range(NY):
                for c in range(NC):
                    to_y = (y + OFFSET[c][zl // 2][zl % 2][x // 2]) % NY
                    source = ((x * NZL + zl) * NY + y) * NC + c
                    pairs.append((source, (TRIPLE[y][c] * NY + to_y) * NC + x % 2))
    return pairs


def encode(blocks, put):
    row = lax.broadcasted_iota(jnp.int32, (TILE, LANES), 0)
    scales = jnp.zeros((TILE, LANES), jnp.float32)
    for j, value in enumerate(blocks):
        size = jnp.abs(value)
        most = jnp.maximum(jnp.max(size, axis=0, keepdims=True), 2.0**-120)
        e = jnp.ceil(4.0 / math.log(2.0) * jnp.log(most))
        root = jnp.sqrt(size) * (TOP * jnp.exp(e * (-math.log(2.0) / 8)))
        q = jnp.round(jnp.where(value < 0, -root, root))
        put(slice(j * ROWS, (j + 1) * ROWS), q.astype(jnp.int32).astype(jnp.int16))
        scales = jnp.where(row == j, e, scales)
    put(slice(NZH * ROWS, CODED), scales.astype(jnp.int32).astype(jnp.int16))


def decode(ref, *at):
    e = ref[(*at, slice(NZH * ROWS, CODED))].astype(jnp.int32).astype(jnp.float32)
    scales = jnp.exp(e * (math.log(2.0) / 8)) * (1.0 / TOP)
    blocks = []
    for j in range(NZH):
        root = ref[(*at, slice(j * ROWS, (j + 1) * ROWS))].astype(jnp.int32).astype(jnp.float32)
        root = root * scales[j : j + 1]
        blocks.append(root * jnp.abs(root))
    return blocks


def decoded_sum(ref, at):
    total = decode(ref, at[0])
    for i in at[1:]:
        total = [a + b for a, b in zip(total, decode(ref, i))]
    return total


def lane_blocks(value):
    return [value[:, j * LANES : (j + 1) * LANES] for j in range(NZH)]


def store(ref, *at):
    def put(rows, value):
        ref[(*at, rows)] = value

    return put


def triple_kernel(at_ref, *refs):
    out_ref = refs[NZH]
    for i in range(NZH):
        j = lax.rem(i + at_ref[0], NZH)
        out_ref[:, pl.ds(pl.multiple_of(j * LANES, LANES), LANES)] = refs[i][...]


def copy_kernel(in_ref, out_ref):
    out_ref[...] = in_ref[...]


def multiply(pairs, columns_ref, out_ref):
    for side in range(2):
        for i in range(2):
            out = lax.dot_general(
                jnp.concatenate(pairs[side][i], axis=1), columns_ref[...],
                (((0,), (0,)), ((), ())), preferred_element_type=jnp.float32,
            )
            for c in range(NC):
                blocks = lane_blocks(out[c * ROWS : (c + 1) * ROWS])
                encode(blocks, store(out_ref, i * NC + c, side))


def near_kernel(own_ref, one_ref, one_other_ref, two_ref, columns_ref, out_ref):
    pairs = [[ref[c] for c in range(NC)] for ref in (one_ref, own_ref, one_other_ref, two_ref)]
    multiply((pairs[:2], pairs[2:]), columns_ref, out_ref)


def far_kernel(at_ref, two_other_ref, three_ref, three_other_ref, far_ref, far_other_ref, columns_ref, out_ref):
    pairs = [[ref[c] for c in range(NC)] for ref in (two_other_ref, three_ref, three_other_ref)]
    far = [jnp.where(at_ref[1] == c, far_ref[...], far_other_ref[...]) for c in range(NC)]
    multiply((pairs[:2], (far, pairs[2])), columns_ref, out_ref)


def sum_x_kernel(part_ref, *refs):
    out_ref = refs[-1]
    done = out_ref.shape[0] - NC
    for c in range(done):
        out_ref[c] = refs[0][c]
    for c in range(NC):
        total = decoded_sum(part_ref, [x * NC + c for x in range(NX)])
        encode(total, store(out_ref, done + c))


def sum_zl_kernel(part_ref, out_ref):
    encode(decoded_sum(part_ref, range(NZL)), store(out_ref))


def update_kernel(scale, total_ref, old_ref, out_ref):
    for j, total in enumerate(decode(total_ref)):
        at = slice(j * LANES, (j + 1) * LANES)
        out_ref[:, at] = 0.9 * old_ref[:, at] + scale * total


def call(kernel, shape, dtype, flops, *arrays, scalars=False):
    specs = [pl.BlockSpec(memory_space=pltpu.VMEM)] * (len(arrays) - scalars)
    if scalars:
        specs = [pl.BlockSpec(memory_space=pltpu.SMEM)] + specs
    return pl.pallas_call(
        kernel,
        in_specs=specs,
        out_specs=pl.BlockSpec(memory_space=pltpu.VMEM),
        out_shape=jax.ShapeDtypeStruct(shape, dtype),
        compiler_params=pltpu.CompilerParams(vmem_limit_bytes=24 << 20),
        cost_estimate=pl.CostEstimate(flops=flops, bytes_accessed=2_000_000, transcendentals=0),
    )(*arrays)


def exchange(part, axes):
    return lax.all_to_all(part, axes, split_axis=0, concat_axis=0, tiled=True)


def body(activations, sample_rows, old_factor):
    block = activations.at[sample_rows].get(mode="promise_in_bounds")
    k = block.shape[0]
    scale = 0.1 / float(NX * NZL * k)
    at = jnp.stack([lax.axis_index("zh"), lax.axis_index("core")]).astype(jnp.int32)
    ring = [lax.all_gather(block, "core", axis=0)]
    for _ in range(3):
        ring.append(lax.ppermute(ring[-1], ("y", "core"), ring_perm()))
    block, _ = lax.optimization_barrier((block, ring[0]))
    swap = lambda value: lax.ppermute(value, "core", [(0, 1), (1, 0)])
    columns = [lax.ppermute(block, ("zh", "y", "core"), triple_perm(i)) for i in range(NZH)]
    one_other = swap(ring[1])
    columns = call(triple_kernel, (k, 384), jnp.bfloat16, COST[0], at, *columns, scalars=True)
    columns, ring[2] = lax.optimization_barrier((columns, ring[2]))
    far = lax.ppermute(block, "y", [(y, (y + 4) % NY) for y in range(NY)])
    far = call(copy_kernel, (k, LANES), jnp.bfloat16, COST[3], far)
    near = call(
        near_kernel, (NX, NC, CODED, LANES), jnp.int16, COST[1],
        ring[0], ring[1], one_other, ring[2], columns,
    )
    away = call(
        far_kernel, (NX, NC, CODED, LANES), jnp.int16, COST[2],
        at, swap(ring[2]), ring[3], swap(ring[3]), far, swap(far), columns, scalars=True,
    )
    part = []
    for half, out in enumerate((near, away)):
        out = exchange(out.reshape(NX * NC, CODED, LANES), "x")
        part = [call(sum_x_kernel, (NC * (half + 1), CODED, LANES), jnp.int16, 0, out, *part)]
    part = exchange(part[0], "zl")
    total = call(sum_zl_kernel, (CODED, LANES), jnp.int16, 0, part)
    total = lax.ppermute(total, ("x", "zl", "y", "core"), place_perm())
    return call(
        functools.partial(update_kernel, scale), old_factor.shape, jnp.float32, 0, total, old_factor
    )


def solution(mesh):
    fine = Mesh(mesh.devices.reshape(NX, NZL, NZH, NY, NC), AXES)
    dp, tensor = ("x", "zl"), ("zh", "y", "core")
    return jax.shard_map(
        body,
        mesh=fine,
        in_specs=(P(dp, tensor), P(dp), P(tensor, dp)),
        out_specs=P(tensor, dp),
        check_vma=False,
    )
```

```python
import functools
import math

import jax
import jax.numpy as jnp
from jax import lax
from jax.experimental import pallas as pl
from jax.experimental.pallas import tpu as pltpu
from jax.sharding import Mesh
from jax.sharding import PartitionSpec as P

NX, NZL, NZH, NY, NC = 4, 4, 3, 8, 2
AXES = ("x", "zl", "zh", "y", "core")
TRIPLE = ((0, 11), (1, 6), (7, 12), (2, 13), (3, 8), (9, 14), (4, 15), (5, 10))
OFFSET = (((-1, -2), (-3, -4)), ((0, 1), (2, 3)))
LANES = 128
ROWS = 128
TILE = 16
LEAST = 2.0**-120
CODED = NZH * ROWS + TILE
TOP = 32700.0


def triple_perm(i):
    return [
        (3 * TRIPLE[y][c] + (i + zh) % 3, zh * 16 + y * NC + c)
        for zh in range(NZH)
        for y in range(NY)
        for c in range(NC)
    ]


def ring_perm(cores):
    return [
        (y * NC + c, (y + 1 - 2 * c) % NY * NC + c) for y in range(NY) for c in cores
    ]


def place_perm():
    pairs = []
    for x in range(NX):
        for zl in range(NZL):
            for y in range(NY):
                for c in range(NC):
                    to_y = (y + OFFSET[c][zl // 2][x // 2]) % NY
                    source = ((x * NZL + zl) * NY + y) * NC + c
                    pairs.append((source, (TRIPLE[y][zl % 2] * NY + to_y) * NC + x % 2))
    return pairs


def encode(blocks, put):
    row = lax.broadcasted_iota(jnp.int32, (TILE, LANES), 0)
    scales = jnp.zeros((TILE, LANES), jnp.float32)
    for j, value in enumerate(blocks):
        size = jnp.abs(value)
        most = jnp.maximum(jnp.max(size, axis=0, keepdims=True), LEAST)
        e = jnp.ceil(4.0 / math.log(2.0) * jnp.log(most))
        root = size * lax.rsqrt(jnp.maximum(size, LEAST))
        root = root * (TOP * jnp.exp(e * (-math.log(2.0) / 8))) + 0.5
        q = jnp.where(value < 0, -root, root)
        put(slice(j * ROWS, (j + 1) * ROWS), q.astype(jnp.int32).astype(jnp.int16))
        scales = jnp.where(row == j, e, scales)
    put(slice(NZH * ROWS, CODED), scales.astype(jnp.int32).astype(jnp.int16))


def decode(ref, *at):
    e = ref[(*at, slice(NZH * ROWS, CODED))].astype(jnp.int32).astype(jnp.float32)
    scales = jnp.exp(e * (math.log(2.0) / 8)) * (1.0 / TOP)
    blocks = []
    for j in range(NZH):
        root = ref[(*at, slice(j * ROWS, (j + 1) * ROWS))].astype(jnp.int32).astype(jnp.float32)
        root = root * scales[j : j + 1]
        blocks.append(root * jnp.abs(root))
    return blocks


def decoded_sum(ref, at):
    total = decode(ref, at[0])
    for i in at[1:]:
        total = [a + b for a, b in zip(total, decode(ref, i))]
    return total


def lane_blocks(value):
    return [value[:, j * LANES : (j + 1) * LANES] for j in range(NZH)]


def store(ref, *at):
    def put(rows, value):
        ref[(*at, rows)] = value

    return put


def triple_kernel(at_ref, *refs):
    out_ref = refs[NZH]
    for i in range(NZH):
        j = lax.rem(i + at_ref[0], NZH)
        out_ref[:, pl.ds(pl.multiple_of(j * LANES, LANES), LANES)] = refs[i][...]


def product_kernel(at_ref, a0_ref, a1_ref, a2_ref, mine_ref, other_ref, out_ref):
    core = at_ref[1]
    for i, (up_ref, down_ref) in enumerate(((a1_ref, a0_ref), (a2_ref, a1_ref))):
        rows = [jnp.where(core == 0, up_ref[c], down_ref[c]) for c in range(NC)]
        rows = jnp.concatenate(rows, axis=1)
        for columns_ref, cw in ((mine_ref, core), (other_ref, 1 - core)):
            out = lax.dot_general(
                rows, columns_ref[...], (((0,), (0,)), ((), ())), preferred_element_type=jnp.float32
            )
            for c in range(NC):
                encode(lane_blocks(out[c * ROWS : (c + 1) * ROWS]), store(out_ref, i * NC + c, cw))


def sum_x_kernel(part_ref, *refs):
    out_ref = refs[-1]
    done = out_ref.shape[0] - NC
    for c in range(done):
        out_ref[c] = refs[0][c]
    for c in range(NC):
        total = decoded_sum(part_ref, [x * NC + c for x in range(NX)])
        encode(total, store(out_ref, done + c))


def sum_zl_kernel(part_ref, out_ref):
    encode(decoded_sum(part_ref, range(NZL)), store(out_ref))


def update_kernel(scale, total_ref, old_ref, out_ref):
    for j, total in enumerate(decode(total_ref)):
        at = slice(j * LANES, (j + 1) * LANES)
        out_ref[:, at] = 0.9 * old_ref[:, at] + scale * total


def call(kernel, shape, dtype, flops, *arrays, scalars=False):
    specs = [pl.BlockSpec(memory_space=pltpu.VMEM)] * (len(arrays) - scalars)
    if scalars:
        specs = [pl.BlockSpec(memory_space=pltpu.SMEM)] + specs
    return pl.pallas_call(
        kernel,
        in_specs=specs,
        out_specs=pl.BlockSpec(memory_space=pltpu.VMEM),
        out_shape=jax.ShapeDtypeStruct(shape, dtype),
        compiler_params=pltpu.CompilerParams(vmem_limit_bytes=24 << 20),
        cost_estimate=pl.CostEstimate(flops=flops, bytes_accessed=2_000_000, transcendentals=0),
    )(*arrays)


def exchange(part, axes):
    return lax.all_to_all(part, axes, split_axis=0, concat_axis=0, tiled=True)


def body(activations, sample_rows, old_factor):
    block = activations.at[sample_rows].get(mode="promise_in_bounds")
    k = block.shape[0]
    scale = 0.1 / float(NX * NZL * k)
    at = jnp.stack([lax.axis_index("zh"), lax.axis_index("core")]).astype(jnp.int32)
    ring = [lax.all_gather(block, "core", axis=0)]
    for step in range(4):
        ring.append(lax.ppermute(ring[-1], ("y", "core"), ring_perm((0, 1) if step < 3 else (0,))))
    block, _ = lax.optimization_barrier((block, ring[0]))
    mine = [lax.ppermute(block, ("zh", "y", "core"), triple_perm(i)) for i in range(NZH)]
    mine = call(triple_kernel, (k, 384), jnp.bfloat16, 10**10, at, *mine, scalars=True)
    mine, ring[2] = lax.optimization_barrier((mine, ring[2]))
    other = lax.ppermute(mine, "core", [(0, 1), (1, 0)])
    part = []
    for half in range(2):
        out = call(
            product_kernel, (NX, NC, CODED, LANES), jnp.int16, 2 * k * 512 * 768,
            at, *ring[2 * half : 2 * half + 3], mine, other, scalars=True,
        )
        out = exchange(out.reshape(NX * NC, CODED, LANES), "x")
        part = [call(sum_x_kernel, (NC * (half + 1), CODED, LANES), jnp.int16, 0, out, *part)]
    part = exchange(part[0], "zl")
    total = call(sum_zl_kernel, (CODED, LANES), jnp.int16, 0, part)
    total = lax.ppermute(total, ("x", "zl", "y", "core"), place_perm())
    return call(
        functools.partial(update_kernel, scale), old_factor.shape, jnp.float32, 0, total, old_factor
    )


def solution(mesh):
    fine = Mesh(mesh.devices.reshape(NX, NZL, NZH, NY, NC), AXES)
    dp, tensor = ("x", "zl"), ("zh", "y", "core")
    return jax.shard_map(
        body,
        mesh=fine,
        in_specs=(P(dp, tensor), P(dp), P(tensor, dp)),
        out_specs=P(tensor, dp),
        check_vma=False,
    )
```

```python
import functools
import math

import jax
import jax.numpy as jnp
from jax import lax
from jax.experimental import pallas as pl
from jax.experimental.pallas import tpu as pltpu
from jax.sharding import Mesh
from jax.sharding import PartitionSpec as P

NX, NZL, NZH, NY, NC = 4, 4, 3, 8, 2
AXES = ("x", "zl", "zh", "y", "core")
TRIPLE = ((0, 11), (1, 6), (7, 12), (2, 13), (3, 8), (9, 14), (4, 10), (5, 15))
OFFSET = (((-1, -2), (-3, -4)), ((0, 1), (2, 3)))
LANES = 128
ROWS = 128
TILE = 16
LEAST = 2.0**-120
CODED = NZH * ROWS + TILE
TOP = 32700.0


def triple_perm(i):
    return [
        (3 * TRIPLE[y][c] + (i + zh) % 3, zh * 16 + y * NC + c)
        for zh in range(NZH)
        for y in range(NY)
        for c in range(NC)
    ]


def ring_perm(cores):
    return [
        (y * NC + c, (y + 1 - 2 * c) % NY * NC + c) for y in range(NY) for c in cores
    ]


def place_perm():
    pairs = []
    for x in range(NX):
        for zl in range(NZL):
            for y in range(NY):
                for c in range(NC):
                    to_y = (y + OFFSET[c][zl // 2][x // 2]) % NY
                    source = ((x * NZL + zl) * NY + y) * NC + c
                    pairs.append((source, (TRIPLE[y][zl % 2] * NY + to_y) * NC + x % 2))
    return pairs


def encode(blocks, put):
    row = lax.broadcasted_iota(jnp.int32, (TILE, LANES), 0)
    scales = jnp.zeros((TILE, LANES), jnp.float32)
    for j, value in enumerate(blocks):
        size = jnp.abs(value)
        most = jnp.maximum(jnp.max(size, axis=0, keepdims=True), LEAST)
        e = jnp.ceil(4.0 / math.log(2.0) * jnp.log(most))
        root = size * lax.rsqrt(jnp.maximum(size, LEAST))
        root = root * (TOP * jnp.exp(e * (-math.log(2.0) / 8))) + 0.5
        q = jnp.where(value < 0, -root, root)
        put(slice(j * ROWS, (j + 1) * ROWS), q.astype(jnp.int32).astype(jnp.int16))
        scales = jnp.where(row == j, e, scales)
    put(slice(NZH * ROWS, CODED), scales.astype(jnp.int32).astype(jnp.int16))


def decode(ref, *at):
    e = ref[(*at, slice(NZH * ROWS, CODED))].astype(jnp.int32).astype(jnp.float32)
    scales = jnp.exp(e * (math.log(2.0) / 8)) * (1.0 / TOP)
    blocks = []
    for j in range(NZH):
        root = ref[(*at, slice(j * ROWS, (j + 1) * ROWS))].astype(jnp.int32).astype(jnp.float32)
        root = root * scales[j : j + 1]
        blocks.append(root * jnp.abs(root))
    return blocks


def decoded_sum(ref, at):
    total = decode(ref, at[0])
    for i in at[1:]:
        total = [a + b for a, b in zip(total, decode(ref, i))]
    return total


def lane_blocks(value):
    return [value[:, j * LANES : (j + 1) * LANES] for j in range(NZH)]


def store(ref, *at):
    def put(rows, value):
        ref[(*at, rows)] = value

    return put


def triple_kernel(at_ref, *refs):
    out_ref = refs[NZH]
    for i in range(NZH):
        j = lax.rem(i + at_ref[0], NZH)
        out_ref[:, pl.ds(pl.multiple_of(j * LANES, LANES), LANES)] = refs[i][...]


def product_kernel(at_ref, a0_ref, a1_ref, a2_ref, mine_ref, other_ref, out_ref):
    core = at_ref[1]
    for i, (up_ref, down_ref) in enumerate(((a1_ref, a0_ref), (a2_ref, a1_ref))):
        rows = [jnp.where(core == 0, up_ref[c], down_ref[c]) for c in range(NC)]
        rows = jnp.concatenate(rows, axis=1)
        for columns_ref, cw in ((mine_ref, core), (other_ref, 1 - core)):
            out = lax.dot_general(
                rows, columns_ref[...], (((0,), (0,)), ((), ())), preferred_element_type=jnp.float32
            )
            for c in range(NC):
                encode(lane_blocks(out[c * ROWS : (c + 1) * ROWS]), store(out_ref, i * NC + c, cw))


def sum_x_kernel(part_ref, *refs):
    out_ref = refs[-1]
    done = out_ref.shape[0] - NC
    for c in range(done):
        out_ref[c] = refs[0][c]
    for c in range(NC):
        total = decoded_sum(part_ref, [x * NC + c for x in range(NX)])
        encode(total, store(out_ref, done + c))


def sum_zl_kernel(part_ref, out_ref):
    encode(decoded_sum(part_ref, range(NZL)), store(out_ref))


def update_kernel(scale, total_ref, old_ref, out_ref):
    for j, total in enumerate(decode(total_ref)):
        at = slice(j * LANES, (j + 1) * LANES)
        out_ref[:, at] = 0.9 * old_ref[:, at] + scale * total


def call(kernel, shape, dtype, flops, *arrays, scalars=False):
    specs = [pl.BlockSpec(memory_space=pltpu.VMEM)] * (len(arrays) - scalars)
    if scalars:
        specs = [pl.BlockSpec(memory_space=pltpu.SMEM)] + specs
    return pl.pallas_call(
        kernel,
        in_specs=specs,
        out_specs=pl.BlockSpec(memory_space=pltpu.VMEM),
        out_shape=jax.ShapeDtypeStruct(shape, dtype),
        compiler_params=pltpu.CompilerParams(vmem_limit_bytes=24 << 20),
        cost_estimate=pl.CostEstimate(flops=flops, bytes_accessed=2_000_000, transcendentals=0),
    )(*arrays)


def exchange(part, axes):
    return lax.all_to_all(part, axes, split_axis=0, concat_axis=0, tiled=True)


def body(activations, sample_rows, old_factor):
    block = activations.at[sample_rows].get(mode="promise_in_bounds")
    k = block.shape[0]
    scale = 0.1 / float(NX * NZL * k)
    at = jnp.stack([lax.axis_index("zh"), lax.axis_index("core")]).astype(jnp.int32)
    ring = [lax.all_gather(block, "core", axis=0)]
    for step in range(4):
        ring.append(lax.ppermute(ring[-1], ("y", "core"), ring_perm((0, 1) if step < 3 else (0,))))
    block, _ = lax.optimization_barrier((block, ring[0]))
    mine = [lax.ppermute(block, ("zh", "y", "core"), triple_perm(i)) for i in range(NZH)]
    mine = call(triple_kernel, (k, 384), jnp.bfloat16, 10**10, at, *mine, scalars=True)
    mine, ring[2] = lax.optimization_barrier((mine, ring[2]))
    other = lax.ppermute(mine, "core", [(0, 1), (1, 0)])
    part = []
    for half in range(2):
        out = call(
            product_kernel, (NX, NC, CODED, LANES), jnp.int16, 2 * k * 512 * 768,
            at, *ring[2 * half : 2 * half + 3], mine, other, scalars=True,
        )
        out = exchange(out.reshape(NX * NC, CODED, LANES), "x")
        part = [call(sum_x_kernel, (NC * (half + 1), CODED, LANES), jnp.int16, 0, out, *part)]
    part = exchange(part[0], "zl")
    total = call(sum_zl_kernel, (CODED, LANES), jnp.int16, 0, part)
    total = lax.ppermute(total, ("x", "zl", "y", "core"), place_perm())
    return call(
        functools.partial(update_kernel, scale), old_factor.shape, jnp.float32, 0, total, old_factor
    )


def solution(mesh):
    fine = Mesh(mesh.devices.reshape(NX, NZL, NZH, NY, NC), AXES)
    dp, tensor = ("x", "zl"), ("zh", "y", "core")
    return jax.shard_map(
        body,
        mesh=fine,
        in_specs=(P(dp, tensor), P(dp), P(tensor, dp)),
        out_specs=P(tensor, dp),
        check_vma=False,
    )
```

```python
import functools
import math

import jax
import jax.numpy as jnp
from jax import lax
from jax.experimental import pallas as pl
from jax.experimental.pallas import tpu as pltpu
from jax.sharding import Mesh
from jax.sharding import PartitionSpec as P

NX, NZL, NZH, NY, NC = 4, 4, 3, 8, 2
AXES = ("x", "zl", "zh", "y", "core")
TRIPLE = ((0, 11), (1, 6), (7, 12), (2, 13), (3, 8), (9, 14), (4, 15), (5, 10))
LANES = 128
ROWS = 128
TILE = 16
LEAST = 2.0**-120
CODED = NZH * ROWS + TILE
TOP = 32700.0


def rows_of(core, half, x):
    if half == 1 and x >= 2:
        return (0 if x == 2 else 4), core
    return (3 if half else 1 + x // 2) * (1 if core else -1), x % 2


def triple_perm(i):
    return [
        (3 * TRIPLE[y][c] + (i + zh) % 3, zh * 16 + y * NC + c)
        for zh in range(NZH)
        for y in range(NY)
        for c in range(NC)
    ]


def ring_perm():
    return [(y * NC + c, (y + 1 - 2 * c) % NY * NC + c) for y in range(NY) for c in range(NC)]


def place_perm():
    pairs = []
    for x in range(NX):
        for zl in range(NZL):
            for y in range(NY):
                for c in range(NC):
                    far, to_c = rows_of(c, zl // 2, x)
                    source = ((x * NZL + zl) * NY + y) * NC + c
                    pairs.append((source, (TRIPLE[y][zl % 2] * NY + (y + far) % NY) * NC + to_c))
    return pairs


def encode(blocks, put):
    row = lax.broadcasted_iota(jnp.int32, (TILE, LANES), 0)
    scales = jnp.zeros((TILE, LANES), jnp.float32)
    for j, value in enumerate(blocks):
        size = jnp.abs(value)
        most = jnp.maximum(jnp.max(size, axis=0, keepdims=True), LEAST)
        e = jnp.ceil(4.0 / math.log(2.0) * jnp.log(most))
        root = size * lax.rsqrt(jnp.maximum(size, LEAST))
        root = root * (TOP * jnp.exp(e * (-math.log(2.0) / 8))) + 0.5
        q = jnp.where(value < 0, -root, root)
        put(slice(j * ROWS, (j + 1) * ROWS), q.astype(jnp.int32).astype(jnp.int16))
        scales = jnp.where(row == j, e, scales)
    put(slice(NZH * ROWS, CODED), scales.astype(jnp.int32).astype(jnp.int16))


def decode(ref, *at):
    e = ref[(*at, slice(NZH * ROWS, CODED))].astype(jnp.int32).astype(jnp.float32)
    scales = jnp.exp(e * (math.log(2.0) / 8)) * (1.0 / TOP)
    blocks = []
    for j in range(NZH):
        root = ref[(*at, slice(j * ROWS, (j + 1) * ROWS))].astype(jnp.int32).astype(jnp.float32)
        root = root * scales[j : j + 1]
        blocks.append(root * jnp.abs(root))
    return blocks


def decoded_sum(ref, at):
    total = decode(ref, at[0])
    for i in at[1:]:
        total = [a + b for a, b in zip(total, decode(ref, i))]
    return total


def lane_blocks(value):
    return [value[:, j * LANES : (j + 1) * LANES] for j in range(NZH)]


def store(ref, *at):
    def put(rows, value):
        ref[(*at, rows)] = value

    return put


def triple_kernel(at_ref, *refs):
    out_ref = refs[NZH]
    for i in range(NZH):
        j = lax.rem(i + at_ref[0], NZH)
        out_ref[:, pl.ds(pl.multiple_of(j * LANES, LANES), LANES)] = refs[i][...]


def product_kernel(at_ref, *refs):
    *row_refs, mine_ref, other_ref, out_ref = refs
    core = at_ref[1]
    rows = []
    for ref in row_refs:
        rows += [ref[...]] if len(ref.shape) == 2 else [ref[c] for c in range(NC)]
    for i in range(0, NX, 2):
        pair = jnp.concatenate(rows[i : i + 2], axis=1)
        for columns_ref, cw in ((mine_ref, core), (other_ref, 1 - core)):
            out = lax.dot_general(
                pair, columns_ref[...], (((0,), (0,)), ((), ())), preferred_element_type=jnp.float32
            )
            for c in range(2):
                encode(lane_blocks(out[c * ROWS : (c + 1) * ROWS]), store(out_ref, i + c, cw))


def sum_x_kernel(part_ref, *refs):
    out_ref = refs[-1]
    done = out_ref.shape[0] - NC
    for c in range(done):
        out_ref[c] = refs[0][c]
    for c in range(NC):
        total = decoded_sum(part_ref, [x * NC + c for x in range(NX)])
        encode(total, store(out_ref, done + c))


def sum_zl_kernel(part_ref, out_ref):
    encode(decoded_sum(part_ref, range(NZL)), store(out_ref))


def update_kernel(scale, total_ref, old_ref, out_ref):
    for j, total in enumerate(decode(total_ref)):
        at = slice(j * LANES, (j + 1) * LANES)
        out_ref[:, at] = 0.9 * old_ref[:, at] + scale * total


def call(kernel, shape, dtype, flops, *arrays, scalars=False):
    specs = [pl.BlockSpec(memory_space=pltpu.VMEM)] * (len(arrays) - scalars)
    if scalars:
        specs = [pl.BlockSpec(memory_space=pltpu.SMEM)] + specs
    return pl.pallas_call(
        kernel,
        in_specs=specs,
        out_specs=pl.BlockSpec(memory_space=pltpu.VMEM),
        out_shape=jax.ShapeDtypeStruct(shape, dtype),
        compiler_params=pltpu.CompilerParams(vmem_limit_bytes=24 << 20),
        cost_estimate=pl.CostEstimate(flops=flops, bytes_accessed=2_000_000, transcendentals=0),
    )(*arrays)


def exchange(part, axes):
    return lax.all_to_all(part, axes, split_axis=0, concat_axis=0, tiled=True)


def body(activations, sample_rows, old_factor):
    block = activations.at[sample_rows].get(mode="promise_in_bounds")
    k = block.shape[0]
    scale = 0.1 / float(NX * NZL * k)
    at = jnp.stack([lax.axis_index("zh"), lax.axis_index("core")]).astype(jnp.int32)
    ring = [lax.all_gather(block, "core", axis=0)]
    for _ in range(3):
        ring.append(lax.ppermute(ring[-1], ("y", "core"), ring_perm()))
    block, _ = lax.optimization_barrier((block, ring[0]))
    mine = [lax.ppermute(block, ("zh", "y", "core"), triple_perm(i)) for i in range(NZH)]
    mine = call(triple_kernel, (k, 384), jnp.bfloat16, 10**10, at, *mine, scalars=True)
    far = lax.ppermute(block, "y", [(y, (y + 4) % NY) for y in range(NY)])
    mine, ring[2], far = lax.optimization_barrier((mine, ring[2], far))
    other = lax.ppermute(mine, "core", [(0, 1), (1, 0)])
    part = []
    for half, rows in enumerate(((ring[1], ring[2]), (ring[3], block, far))):
        out = call(
            product_kernel, (NX, NC, CODED, LANES), jnp.int16, 4 * 10**9,
            at, *rows, mine, other, scalars=True,
        )
        out = exchange(out.reshape(NX * NC, CODED, LANES), "x")
        part = [call(sum_x_kernel, (NC * (half + 1), CODED, LANES), jnp.int16, 0, out, *part)]
    part = exchange(part[0], "zl")
    total = call(sum_zl_kernel, (CODED, LANES), jnp.int16, 0, part)
    total = lax.ppermute(total, ("x", "zl", "y", "core"), place_perm())
    return call(
        functools.partial(update_kernel, scale), old_factor.shape, jnp.float32, 0, total, old_factor
    )


def solution(mesh):
    fine = Mesh(mesh.devices.reshape(NX, NZL, NZH, NY, NC), AXES)
    dp, tensor = ("x", "zl"), ("zh", "y", "core")
    return jax.shard_map(
        body,
        mesh=fine,
        in_specs=(P(dp, tensor), P(dp), P(tensor, dp)),
        out_specs=P(tensor, dp),
        check_vma=False,
    )
```
